512 devices in a mesh: owner: 128 (over y, z, core), rep: 4 (over x).
Axes of the slice: x: 4, y: 8, z: 8, core: 2. Of those that a mesh axis runs over, the one named last changes fastest.
Arguments:
- bin_blocks: int32 [131072], P(('owner', 'rep')), may hold values from 0 to 32767, as said below
- send_counts: int32 [512, 128], P(('owner', 'rep')), may hold values from 0 to 4, as said below
- voxel_index: int32 [131072, 128], P(('owner', 'rep')), may hold values from 0 to 511
- point_sdf: bfloat16 [131072, 128], P(('owner', 'rep')), may hold values from -1 to 1
- point_weight: bfloat16 [131072, 128], P(('owner', 'rep')), may hold values from 0.099609375 to 1
- point_color: bfloat16 [131072, 3, 128], P(('owner', 'rep')), may hold values from 0 to 1
- owner_table: int32 [32768], replicated, may hold values from 0 to 32767, as said below
- old_tsdf: float32 [32768, 4, 512], P(('owner', 'rep')), may hold values from -1 to 1
- old_weight: float32 [32768, 512], P(('owner', 'rep')), may hold values from 0.5 to 4
Outputs:
- new_tsdf: float32 [32768, 4, 512], P(('owner', 'rep'))
- new_weight: float32 [32768, 512], P(('owner', 'rep'))
The draws below stay inside these ranges and needn't reach their ends.
Inputs may be any that keep to these rules, and one draw needn't show every extreme that they name: `send_counts`: each row sums to 256; every row has an entry equal to 4; among the devices s with the same s mod 4 (one frame group), some owner receives 4 bins from every one of them. `owner_table`: a permutation; entry g is the owner of block g times 256 plus the block's place among that owner's blocks. `bin_blocks`: owner_table assigns the block of bin j of device s to owner p(s, j) of the first step; of the bins that one frame group sends to one owner, at most 128 have places in any one quarter of its 256 places (places q * 64 to (q + 1) * 64 - 1), and this most is reached in every frame group.
All inputs are finite; a program needn't handle non-finite values.
Results may differ from the reference program's by a relative error of at most 0.00078.
Values may be sent and summed in bfloat16 or wider, within the bound.
No kernel may reach another device: no remote copies, remote signals or barrier semaphores. Data moves between devices by JAX's collectives and lax.ppermute only.
A program may use at most 64 MiB of HBM per device.

```python
import math
import jax
import jax.numpy as jnp
from jax import lax

BINS = 256
OWN = 256
BLK = 128
VOX = 512
CAP = 4
NBLK = 32768
TOTAL_BINS = 131072
N_OWNER = 128
N_REP = 4


def owner_order(key):
    return jax.random.permutation(jax.random.fold_in(key, 11), OWN * N_OWNER).astype(jnp.int32)


def count_rows(key):
    base_key = jax.random.fold_in(key, 23)
    hot_owners = jax.random.randint(jax.random.fold_in(key, 29), (N_REP,), 0, N_OWNER).astype(jnp.int32)
    owner_ids = jnp.arange(N_OWNER, dtype=jnp.int32)

    def one_device(device_key, device):
        key_order, key_share = jax.random.split(device_key)
        shuffled = jax.random.permutation(key_order, N_OWNER).astype(jnp.int32)
        hot = hot_owners[device % N_REP]
        where_hot = jnp.sum(jnp.where(shuffled == hot, owner_ids, 0)).astype(jnp.int32)
        first_entry = shuffled[0]
        shuffled = shuffled.at[where_hot].set(first_entry)
        shuffled = shuffled.at[0].set(hot)
        first_share = jax.random.randint(key_share, (N_OWNER // 2,), 0, CAP + 1).astype(jnp.int32)
        first_share = first_share.at[0].set(CAP)
        row_counts = jnp.zeros((N_OWNER,), jnp.int32)
        row_counts = row_counts.at[shuffled[0::2]].set(first_share)
        row_counts = row_counts.at[shuffled[1::2]].set(CAP - first_share)
        return row_counts
    device_keys = jax.random.split(base_key, N_OWNER * N_REP)
    devices = jnp.arange(N_OWNER * N_REP, dtype=jnp.int32)
    return jax.vmap(one_device)(device_keys, devices)


def draw_owner_table(key, part):
    return owner_order(key)


def draw_send_counts(key, part):
    return count_rows(key)


def draw_bin_blocks(key, part):
    row_counts = count_rows(key)
    inverse = jnp.argsort(owner_order(key)).astype(jnp.int32)
    running_end = jnp.cumsum(row_counts, axis=1)
    starts = (running_end - row_counts).astype(jnp.int32)
    bin_ids = jnp.arange(BINS, dtype=jnp.int32)
    target = jnp.sum((bin_ids[None, :, None] >= running_end[:, None, :]).astype(jnp.int32), axis=2).astype(jnp.int32)
    grid = row_counts.reshape(N_OWNER, N_REP, N_OWNER)
    before = (jnp.cumsum(grid, axis=0) - grid).reshape(N_OWNER * N_REP, N_OWNER).astype(jnp.int32)
    position = bin_ids[None, :] - jnp.take_along_axis(starts, target, axis=1)
    rank = jnp.take_along_axis(before, target, axis=1) + position
    quarter = rank % N_REP
    share = OWN // N_REP
    offset = jax.random.randint(jax.random.fold_in(key, 37), (N_OWNER * N_REP, BINS), 0, share).astype(jnp.int32)
    local_index = (quarter * share + offset).astype(jnp.int32)
    return inverse[target * OWN + local_index].reshape(-1).astype(jnp.int32)


def place_ends(result, rng, least, high):
    index_at = [jax.random.randint(jax.random.fold_in(rng, axis), (), 0, length) for axis, length in enumerate(result.shape)]
    longest = result.shape.index(max(result.shape))
    beside = index_at[:longest] + [(index_at[longest] + 1) % result.shape[longest]] + index_at[longest + 1:]
    return result.at[tuple(index_at)].set(least).at[tuple(beside)].set(high)


def shard_levels(key, extent, cuts, smallest, high):
    loudness, own = 1.0, jax.random.fold_in(key, 6)
    for dim, blocks in cuts:
        draws = jnp.exp(jax.random.uniform(jax.random.fold_in(own, dim), (blocks,), jnp.float32, smallest / len(cuts), high / len(cuts)))
        loudness = loudness * jnp.repeat(draws, extent[dim] // blocks).reshape([-1 if axis == dim else 1 for axis in range(len(extent))])
    return loudness


def setup_inputs(seed: int = 0) -> dict:
    key_list = jax.random.split(jax.random.key(seed), 10)
    bin_blocks = draw_bin_blocks(jax.random.fold_in(key_list[9], 71), 0)
    send_counts = draw_send_counts(jax.random.fold_in(key_list[9], 71), 0)
    voxel_index = place_ends(jax.random.randint(key_list[2], (TOTAL_BINS, BLK), 0, VOX), jax.random.fold_in(key_list[2], 1), 0, VOX - 1).astype(jnp.int32)
    point_sdf = jnp.clip(jax.random.uniform(key_list[3], (TOTAL_BINS, BLK), jnp.float32, -1.0, 1.0) * shard_levels(key_list[3], (TOTAL_BINS, BLK), ((0, 512),), -0.4, 0.0), -1.0, 1.0).astype(jnp.bfloat16)
    point_weight = jnp.clip(jnp.exp(math.log(1.0) - 2.306499 * jax.random.uniform(key_list[4], (TOTAL_BINS, BLK), jnp.float32) ** shard_levels(key_list[4], (TOTAL_BINS, BLK), ((0, 512),), -0.2, 0.2)), 0.099609375, 1.0).astype(jnp.bfloat16)
    point_color = jnp.clip(1.0 * jax.random.uniform(key_list[5], (TOTAL_BINS, 3, BLK), jnp.float32) ** shard_levels(key_list[5], (TOTAL_BINS, 3, BLK), ((0, 512),), -0.2, 0.2), 0.0, 1.0).astype(jnp.bfloat16)
    owner_table = draw_owner_table(jax.random.fold_in(key_list[9], 71), 0)
    old_tsdf = jnp.clip(jax.random.uniform(key_list[7], (NBLK, 4, VOX), jnp.float32, -1.0, 1.0) * shard_levels(key_list[7], (NBLK, 4, VOX), ((0, 512),), -0.4, 0.0), -1.0, 1.0)
    old_weight = jnp.clip(jnp.exp(math.log(4.0) - 2.0794415 * jax.random.uniform(key_list[8], (NBLK, VOX), jnp.float32) ** shard_levels(key_list[8], (NBLK, VOX), ((0, 512),), -0.2, 0.2)), 0.5, 4.0)
    return dict(bin_blocks=bin_blocks, send_counts=send_counts, voxel_index=voxel_index, point_sdf=point_sdf, point_weight=point_weight, point_color=point_color, owner_table=owner_table, old_tsdf=old_tsdf, old_weight=old_weight)


def reference(bin_blocks, send_counts, voxel_index, point_sdf, point_weight, point_color, owner_table, old_tsdf, old_weight):
    running_end = jnp.cumsum(send_counts, axis=1)
    bin_ids = jnp.arange(BINS, dtype=jnp.int32)
    target = jnp.sum((bin_ids[None, :, None] >= running_end[:, None, :]).astype(jnp.int32), axis=2).reshape(-1)
    local_index = (owner_table[bin_blocks] % OWN).astype(jnp.int32)
    block_index = (target * OWN + local_index).astype(jnp.int32)
    cell_index = (block_index[:, None] * VOX + voxel_index).astype(jnp.int32)
    pieces = 8

    def add_piece(sums_now, span):
        cells, weight_raw, sdf_raw, color_raw = span
        weight = weight_raw.astype(jnp.float32)
        weighted_sdf = lax.optimization_barrier((weight * sdf_raw.astype(jnp.float32)).astype(jnp.bfloat16)).astype(jnp.float32)
        weighted_color = lax.optimization_barrier((weight[:, None, :] * color_raw.astype(jnp.float32)).astype(jnp.bfloat16)).astype(jnp.float32)
        values = jnp.concatenate([weight[:, None, :], weighted_sdf[:, None, :], weighted_color], axis=1)
        flat = jnp.transpose(values, (0, 2, 1)).reshape(-1, 5)
        return sums_now.at[cells.reshape(-1)].add(flat), None

    sums_start = jnp.zeros((NBLK * VOX, 5), jnp.float32)
    spans = (cell_index.reshape(pieces, -1, BLK), point_weight.reshape(pieces, -1, BLK),
              point_sdf.reshape(pieces, -1, BLK), point_color.reshape(pieces, -1, 3, BLK))
    sums_end, _ = lax.scan(add_piece, sums_start, spans)
    sums_cell = jnp.transpose(sums_end.reshape(NBLK, VOX, 5), (0, 2, 1))
    new_weight = old_weight + sums_cell[:, 0]
    joined_sdf = (old_weight * old_tsdf[:, 0] + sums_cell[:, 1]) / new_weight
    joined_color = (old_weight[:, None, :] * old_tsdf[:, 1:] + sums_cell[:, 2:]) / new_weight[:, None, :]
    new_tsdf = jnp.concatenate([joined_sdf[:, None, :], joined_color], axis=1)
    return new_tsdf, new_weight
```

```python
import functools
import jax, jax.numpy as jnp
from jax import lax
from jax.experimental import pallas as pl
from jax.experimental.pallas import tpu as pltpu
from jax.sharding import PartitionSpec as P
bf16=jnp.bfloat16; f32=jnp.float32; i32=jnp.int32
OWN=256
def row_ids(shape,dim): return lax.broadcasted_iota(i32,shape,dim)

def pack_kernel(counts_ref, blocks_ref, table_ref, voxel_ref, sdf_ref, weight_ref, color_ref, out_ref):
    owners=counts_ref.shape[1]; bins=blocks_ref.shape[1]
    counts=jnp.broadcast_to(counts_ref[...],(owners,owners)).astype(f32)
    up=row_ids((owners,owners),0); across=row_ids((owners,owners),1)
    ends=jnp.sum(jnp.where(across<=up,counts,0.0),axis=1,keepdims=True)
    own=jnp.sum(jnp.where(across==up,counts,0.0),axis=1,keepdims=True)
    bin_ids=row_ids((owners,bins),1).astype(f32)
    passed=bin_ids>=ends
    target=jnp.sum(jnp.where(passed,1.0,0.0),axis=0,keepdims=True)
    before=jnp.sum(jnp.where(passed,own,0.0),axis=0,keepdims=True)
    slot=(8.0*target+bin_ids[:1]-before).astype(i32)
    blocks=blocks_ref[...]
    trows=table_ref.shape[0]
    pick=jnp.where(row_ids((trows,bins),0)==blocks//128,1.0,0.0).astype(bf16)
    table=(table_ref[...]%OWN).astype(f32).astype(bf16)
    found=lax.dot_general(table,pick,(((0,),(0,)),((),())),preferred_element_type=f32)
    place=jnp.sum(jnp.where(row_ids((128,bins),0)==blocks%128,found,0.0),axis=0,keepdims=True)+1.0
    select=jnp.where(row_ids((8*owners,bins),0)==slot,1.0,0.0).astype(bf16)
    def put(c,values):
        out_ref[:,:,c*128:(c+1)*128]=values.reshape(owners,8,128)[:,:4].astype(bf16)
    weight=weight_ref[...].astype(f32)
    feats=[(voxel_ref[...]-256).astype(f32).astype(bf16),weight_ref[...],(weight*sdf_ref[...].astype(f32)).astype(bf16)]
    feats+=[(weight*color_ref[c].astype(f32)).astype(bf16) for c in range(3)]
    for c in range(0,6,2):
        got=jnp.dot(select,jnp.concatenate(feats[c:c+2],axis=1),preferred_element_type=f32)
        put(c,got[:,:128]); put(c+1,got[:,128:])
    put(6,lax.dot_general(select,jnp.broadcast_to(place,(128,bins)).astype(bf16),(((1,),(1,)),((),())),preferred_element_type=f32))

def pack(counts,blocks,table,voxel,sdf,weight,color):
    owners=counts.shape[1]
    return pl.pallas_call(pack_kernel,out_shape=jax.ShapeDtypeStruct((owners,4,7*128),bf16),
        compiler_params=pltpu.CompilerParams(vmem_limit_bytes=48<<20),name="pack")(counts,blocks.reshape(1,-1),table.reshape(-1,128),voxel,sdf,weight,color.transpose(1,0,2))

def rows_of(ref,c):
    x=ref[:,:,c*128:(c+1)*128]
    return x.reshape(4*x.shape[0],128)

def route_kernel(replicas,in_ref,out_ref):
    quota=out_ref.shape[0]//replicas
    share=OWN//replicas
    codes=rows_of(in_ref,6)
    n=codes.shape[0]
    eye=jnp.where(row_ids((128,128),0)==row_ids((128,128),1),1.0,0.0)
    lower=jnp.where(row_ids((128,128),0)<row_ids((128,128),1),1.0,0.0).astype(bf16)
    quarters=row_ids((8,128),0).astype(f32)
    total=jnp.zeros((8,1),f32)
    dests=[]
    for g in range(n//128):
        code=jnp.sum(codes[g*128:(g+1)*128].astype(f32)*eye,axis=0,keepdims=True)
        live=code>0.5
        quarter=jnp.where(live,jnp.floor((code-1.0)*(1.0/share)),9.0)
        member=jnp.where(quarters==quarter,1.0,0.0)
        ahead=jnp.dot(member.astype(bf16),lower,preferred_element_type=f32)+total
        total=total+jnp.sum(member,axis=1,keepdims=True)
        rank=jnp.sum(ahead*member,axis=0,keepdims=True)
        dests.append(jnp.where(live,quarter*quota+rank,-1.0))
    dest=jnp.concatenate(dests,axis=1).astype(i32)
    select=jnp.where(row_ids((replicas*quota,n),0)==dest,1.0,0.0).astype(bf16)
    for c in range(0,7,2):
        w=min(2,7-c)
        x=jnp.concatenate([rows_of(in_ref,c+k) for k in range(w)],axis=1)
        out_ref[:,c*128:(c+w)*128]=jnp.dot(select,x,preferred_element_type=f32).astype(bf16)

def route(x,replicas):
    bins=x.shape[0]*2
    quota=2*bins//replicas
    return pl.pallas_call(functools.partial(route_kernel,replicas),out_shape=jax.ShapeDtypeStruct((replicas*quota,7*128),bf16),
        compiler_params=pltpu.CompilerParams(vmem_limit_bytes=48<<20),name="route")(x)

GROUP=16
def join_kernel(pair,in_ref,tsdf_ref,weight_ref,new_tsdf_ref,new_weight_ref,acc_ref,codes_ref,code_smem,sem):
    rows=in_ref.shape[0]; places=weight_ref.shape[0]
    share=places
    sources=rows//128
    acc_ref[...]=jnp.zeros_like(acc_ref)
    eye=jnp.where(row_ids((128,128),0)==row_ids((128,128),1),1.0,0.0)
    for r in range(sources):
        code=jnp.sum(in_ref[r*128:(r+1)*128,6*128:7*128].astype(f32)*eye,axis=0,keepdims=True)
        spot=code-1.0
        spot=spot-jnp.floor(spot*(1.0/share))*share
        codes_ref[r:r+1,:]=jnp.where(code>0.5,spot,0.0).astype(i32)
        live=jnp.sum(jnp.where(code>0.5,1.0,0.0),axis=1,keepdims=True)
        codes_ref[sources+r:sources+r+1,:]=jnp.broadcast_to(live,(1,128)).astype(i32)
    copy=pltpu.make_async_copy(codes_ref,code_smem,sem); copy.start(); copy.wait()
    lanes=row_ids((128,128),0).astype(f32).astype(bf16)
    sub=row_ids((8,128),0)
    def group(r,base):
        start=pl.multiple_of(r*128+base*GROUP,GROUP)
        tiles=[in_ref[pl.ds(start,GROUP),c*128:(c+1)*128].astype(f32) for c in range(6)]
        voxel=tiles[0]+256.0
        upper=jnp.floor(voxel*(1.0/128.0)); lower=(voxel-upper*128.0).astype(bf16)
        def parts(b):
            hot=jnp.where(lanes==jnp.broadcast_to(lower[b:b+1],(128,128)),jnp.ones((),bf16),jnp.zeros((),bf16))
            feat=jnp.zeros((8,128),f32)
            for c in range(5): feat=jnp.where(sub==c,jnp.broadcast_to(tiles[1+c][b:b+1],(8,128)),feat)
            up=jnp.broadcast_to(upper[b:b+1],(8,128))
            left=jnp.concatenate([jnp.where(up==a,feat,0.0) for a in range(4)],axis=0).astype(bf16)
            return hot,left
        def add(b,grid):
            place=code_smem[r,base*GROUP+b]
            at=pl.ds(pl.multiple_of(place*32,32),32)
            acc_ref[at,:]+=grid
        if pair==1:
            for b in range(GROUP):
                hot,left=parts(b)
                add(b,lax.dot_general(left,hot,(((1,),(1,)),((),())),preferred_element_type=f32))
        else:
            for b in range(0,GROUP,2):
                h0,l0=parts(b); h1,l1=parts(b+1)
                z=jnp.zeros_like(l0)
                left=jnp.concatenate([jnp.concatenate([l0,z],axis=1),jnp.concatenate([z,l1],axis=1)],axis=0)
                g=lax.dot_general(left,jnp.concatenate([h0,h1],axis=1),(((1,),(1,)),((),())),preferred_element_type=f32)
                add(b,g[:32]); add(b+1,g[32:])
    for r in range(sources):
        n=(code_smem[sources+r,0]+GROUP-1)//GROUP
        def body(base,carry):
            group(r,base); return carry
        lax.fori_loop(0,n,body,0)
    for a in range(4):
        cols=slice(a*128,(a+1)*128)
        old=weight_ref[:,cols]
        new=old+acc_ref[pl.ds(a*8,places,stride=32),:]
        new_weight_ref[:,cols]=new
        for c in range(4):
            new_tsdf_ref[:,c,cols]=(old*tsdf_ref[:,c,cols]+acc_ref[pl.ds(a*8+1+c,places,stride=32),:])/new

def join(x,old_tsdf,old_weight,pair=2):
    places=old_weight.shape[0]; sources=x.shape[0]//128
    return pl.pallas_call(functools.partial(join_kernel,pair),
        out_shape=(jax.ShapeDtypeStruct(old_tsdf.shape,f32),jax.ShapeDtypeStruct(old_weight.shape,f32)),
        scratch_shapes=[pltpu.VMEM((places*32,128),f32),pltpu.VMEM((2*sources,128),i32),pltpu.SMEM((2*sources,128),i32),pltpu.SemaphoreType.DMA(())],
        compiler_params=pltpu.CompilerParams(vmem_limit_bytes=48<<20),name="join")(x,old_tsdf,old_weight)


def local(bin_blocks,send_counts,voxel_index,point_sdf,point_weight,point_color,owner_table,old_tsdf,old_weight):
    packed=pack(send_counts,bin_blocks,owner_table,voxel_index,point_sdf,point_weight,point_color)
    arrived=lax.all_to_all(packed,"owner",split_axis=0,concat_axis=0,tiled=True)
    sent=route(arrived,lax.axis_size("rep"))
    final=lax.all_to_all(sent,"rep",split_axis=0,concat_axis=0,tiled=True)
    return join(final,old_tsdf,old_weight)


def solution(mesh):
    both=("owner","rep")
    placed=(P(both),P(both,None),P(both,None),P(both,None),P(both,None),P(both,None,None),P(),P(both,None,None),P(both,None))
    return jax.shard_map(local,mesh=mesh,in_specs=placed,out_specs=(P(both,None,None),P(both,None)),check_vma=False)
```

```python
import functools

import jax
import jax.numpy as jnp
from jax import lax
from jax.experimental import pallas as pl
from jax.experimental.pallas import tpu as pltpu
from jax.sharding import PartitionSpec as P

bf16 = jnp.bfloat16
f32 = jnp.float32
i32 = jnp.int32
OWN = 256
LANES = 128
UNIT = 8
WIDE = 8
PARAMS = pltpu.CompilerParams(vmem_limit_bytes=48 << 20)


def ids(shape, dim):
    return lax.broadcasted_iota(i32, shape, dim)


def dot(a, b, dims=((1,), (0,))):
    return lax.dot_general(a, b, (dims, ((), ())), preferred_element_type=f32)


def pack_kernel(*refs):
    sources, out_ref, held, sems = refs[:7], refs[7], refs[8:15], refs[15]
    copies = [
        pltpu.make_async_copy(a, b, sems.at[n]) for n, (a, b) in enumerate(zip(sources, held))
    ]
    for copy in copies:
        copy.start()
    counts_ref, blocks_ref, table_ref, voxel_ref, weight_ref, sdf_ref, color_ref = held
    owners = counts_ref.shape[1]
    bins = blocks_ref.shape[1]
    copies[0].wait()
    counts = jnp.broadcast_to(counts_ref[...], (owners, owners)).astype(f32)
    row, lane = ids((owners, owners), 0), ids((owners, owners), 1)
    ends = jnp.sum(jnp.where(lane <= row, counts, 0.0), axis=1, keepdims=True)
    own = jnp.sum(jnp.where(lane == row, counts, 0.0), axis=1, keepdims=True)
    bin_ids = ids((owners, bins), 1).astype(f32)
    passed = bin_ids >= ends
    target = jnp.sum(jnp.where(passed, 1.0, 0.0), axis=0, keepdims=True)
    before = jnp.sum(jnp.where(passed, own, 0.0), axis=0, keepdims=True)
    slot = (8.0 * target + bin_ids[:1] - before).astype(i32)
    select = jnp.where(ids((8 * owners, bins), 0) == slot, 1.0, 0.0).astype(bf16)
    copies[1].wait()
    copies[2].wait()
    blocks = blocks_ref[...]
    pick = jnp.where(ids((table_ref.shape[0], bins), 0) == blocks // LANES, 1.0, 0.0).astype(bf16)
    table = (table_ref[...] % OWN).astype(f32).astype(bf16)
    found = dot(table, pick, ((0,), (0,)))
    code = 1.0 + jnp.sum(
        jnp.where(ids((LANES, bins), 0) == blocks % LANES, found, 0.0), axis=0, keepdims=True
    )

    def put(channel, values):
        cut = values.reshape(owners, 8, LANES)[:, :4].astype(bf16)
        out_ref[:, :, channel * LANES : (channel + 1) * LANES] = cut

    put(6, dot(select, jnp.broadcast_to(code, (LANES, bins)).astype(bf16), ((1,), (1,))))
    for copy in copies[3:]:
        copy.wait()
    weight = weight_ref[...].astype(f32)
    features = [(voxel_ref[...] - 256).astype(f32).astype(bf16), weight_ref[...]]
    features.append((weight * sdf_ref[...].astype(f32)).astype(bf16))
    features += [(weight * color_ref[c].astype(f32)).astype(bf16) for c in range(3)]
    for c in range(0, 6, 2):
        pair = dot(select, jnp.concatenate(features[c : c + 2], axis=1))
        put(c, pair[:, :LANES])
        put(c + 1, pair[:, LANES:])


def pack(counts, blocks, table, voxel, weight, sdf, color):
    arrays = (
        counts,
        blocks.reshape(1, -1),
        table.reshape(-1, LANES),
        voxel,
        weight,
        sdf,
        color.transpose(1, 0, 2),
    )
    return pl.pallas_call(
        pack_kernel,
        out_shape=jax.ShapeDtypeStruct((counts.shape[1], 4, 7 * LANES), bf16),
        in_specs=[pl.BlockSpec(memory_space=pltpu.HBM)] * len(arrays),
        scratch_shapes=[pltpu.VMEM(a.shape, a.dtype) for a in arrays]
        + [pltpu.SemaphoreType.DMA((len(arrays),))],
        compiler_params=PARAMS,
        name="pack",
    )(*(pltpu.with_memory_space_constraint(a, pltpu.HBM) for a in arrays))


def rows_of(ref, channel):
    part = ref[:, :, channel * LANES : (channel + 1) * LANES]
    return part.reshape(4 * part.shape[0], LANES)


def route_kernel(in_ref, out_ref):
    replicas, height = out_ref.shape[:2]
    quota = height - 8
    share = OWN // replicas
    codes = rows_of(in_ref, 6)
    count = codes.shape[0]
    eye = jnp.where(ids((LANES, LANES), 0) == ids((LANES, LANES), 1), 1.0, 0.0)
    earlier = jnp.where(ids((LANES, LANES), 0) < ids((LANES, LANES), 1), 1.0, 0.0).astype(bf16)
    quarters = ids((8, LANES), 0).astype(f32)
    total = jnp.zeros((8, 1), f32)
    destinations, spots = [], []
    for g in range(count // LANES):
        block = codes[g * LANES : (g + 1) * LANES].astype(f32)
        code = jnp.sum(block * eye, axis=0, keepdims=True)
        live = code > 0.5
        quarter = jnp.where(live, jnp.floor((code - 1.0) * (1.0 / share)), 9.0)
        member = jnp.where(quarters == quarter, 1.0, 0.0)
        ahead = dot(member.astype(bf16), earlier) + total
        total = total + jnp.sum(member, axis=1, keepdims=True)
        rank = jnp.sum(ahead * member, axis=0, keepdims=True)
        destinations.append(jnp.where(live, quarter * quota + rank, -1.0))
        spots.append(jnp.where(live, code - quarter * share, 0.0))
    destination = jnp.concatenate(destinations, axis=1).astype(i32)
    spot = jnp.concatenate(spots, axis=1)
    select = jnp.where(ids((replicas * quota, count), 0) == destination, 1.0, 0.0).astype(bf16)
    placed = dot(jnp.broadcast_to(spot, (8, count)).astype(bf16), select, ((1,), (1,)))
    for q in range(replicas):
        out_ref[q, quota:, :LANES] = placed[:, q * quota : (q + 1) * quota].astype(bf16)
        out_ref[q, quota:, LANES:] = jnp.zeros((8, out_ref.shape[2] - LANES), bf16)
    for c in range(0, 6, 2):
        pair = jnp.concatenate([rows_of(in_ref, c), rows_of(in_ref, c + 1)], axis=1)
        moved = dot(select, pair).astype(bf16)
        for q in range(replicas):
            out_ref[q, :quota, c * LANES : (c + 2) * LANES] = moved[q * quota : (q + 1) * quota]


def route(arrived, replicas):
    quota = 4 * arrived.shape[0] // replicas
    return pl.pallas_call(
        route_kernel,
        out_shape=jax.ShapeDtypeStruct((replicas, quota + 8, 6 * LANES), bf16),
        compiler_params=PARAMS,
        name="route",
    )(arrived)


def join_kernel(
    in_ref, tsdf_ref, weight_ref, new_tsdf_hbm, new_weight_hbm,
    sums_ref, new_tsdf_ref, new_weight_ref, plan_ref, plan, sem, sems,
):
    places = weight_ref.shape[0]
    height = 136
    quota = height - 8
    groups = in_ref.shape[0] // height
    units = groups * quota // UNIT
    unit_row, unit_lane = ids((LANES, LANES), 0), ids((LANES, LANES), 1)
    live_units = jnp.zeros((LANES, LANES), f32)
    for r in range(groups):
        code = in_ref[r * height + quota : r * height + height, :LANES].astype(f32)[:1]
        live = jnp.where(code > 0.5, 1.0, 0.0)
        plan_ref[r : r + 1, :] = jnp.where(code > 0.5, code - 1.0, float(places)).astype(i32)
        bins = jnp.sum(live, axis=1, keepdims=True)
        first = ((unit_row - r * (quota // UNIT)) * UNIT).astype(f32)
        here = (unit_row >= r * (quota // UNIT)) & (unit_row < (r + 1) * (quota // UNIT))
        live_units = jnp.where(here & (first < bins), 1.0, live_units)
    plan_ref[groups : groups + 1, :] = jnp.full((1, LANES), places, i32)
    below = jnp.where(unit_lane < unit_row, 1.0, 0.0).astype(bf16)
    rank = dot(below, live_units.astype(bf16))
    chosen = (live_units > 0.5) & (rank == unit_lane.astype(f32))
    listed = jnp.sum(jnp.where(chosen, unit_row.astype(f32) + 1.0, 0.0), axis=0, keepdims=True)
    listed = jnp.where(listed > 0.5, listed - 1.0, float(units))
    plan_ref[groups + 1 : groups + 2, :] = listed.astype(i32)
    number = jnp.sum(live_units, axis=0, keepdims=True)
    plan_ref[groups + 2 : groups + 3, :] = number.astype(i32)
    copy = pltpu.make_async_copy(plan_ref, plan, sem)
    copy.start()
    sums_ref[...] = jnp.zeros_like(sums_ref)
    copy.wait()

    lanes = ids((LANES, LANES), 0).astype(f32).astype(bf16)
    sub = ids((8, LANES), 0)
    one, zero = jnp.ones((), bf16), jnp.zeros((), bf16)

    def halves(tiles, upper, lower, b):
        hot = jnp.where(lanes == jnp.broadcast_to(lower[b : b + 1], (LANES, LANES)), one, zero)
        feature = jnp.zeros((8, LANES), f32)
        for c in range(5):
            value = jnp.broadcast_to(tiles[1 + c][b : b + 1], (8, LANES))
            feature = jnp.where(sub == c, value, feature)
        level = jnp.broadcast_to(upper[b : b + 1], (8, LANES))
        left = [jnp.where(level == a, feature, 0.0) for a in range(4)]
        return hot, jnp.concatenate(left, axis=0).astype(bf16)

    def step(n, carry):
        for u in range(WIDE):
            unit = plan[groups + 1, n * WIDE + u]
            group = unit // (quota // UNIT)
            within = (unit % (quota // UNIT)) * UNIT
            start = jnp.where(unit < units, group * height + within, 0)
            start = pl.multiple_of(start, UNIT)
            tiles = [
                in_ref[pl.ds(start, UNIT), c * LANES : (c + 1) * LANES].astype(f32)
                for c in range(6)
            ]
            voxel = tiles[0] + 256.0
            upper = jnp.floor(voxel * (1.0 / LANES))
            lower = (voxel - upper * float(LANES)).astype(bf16)
            for b in range(0, UNIT, 2):
                hot_a, left_a = halves(tiles, upper, lower, b)
                hot_b, left_b = halves(tiles, upper, lower, b + 1)
                empty = jnp.zeros_like(left_a)
                left = jnp.concatenate(
                    [
                        jnp.concatenate([left_a, empty], axis=1),
                        jnp.concatenate([empty, left_b], axis=1),
                    ],
                    axis=0,
                )
                grids = dot(left, jnp.concatenate([hot_a, hot_b], axis=1), ((1,), (1,)))
                for k in range(2):
                    at = pl.multiple_of(plan[group, within + b + k] * 32, 32)
                    sums_ref[pl.ds(at, 32), :] += grids[k * 32 : (k + 1) * 32]
        return carry

    lax.fori_loop(0, (plan[groups + 2, 0] + WIDE - 1) // WIDE, step, 0)

    copies = []
    for a in range(4):
        cols = slice(a * LANES, (a + 1) * LANES)
        old = weight_ref[:, cols]
        new = old + sums_ref[pl.ds(a * 8, places, stride=32), :]
        new_weight_ref[:, cols] = new
        for c in range(4):
            share = sums_ref[pl.ds(a * 8 + 1 + c, places, stride=32), :]
            new_tsdf_ref[:, c, cols] = (old * tsdf_ref[:, c, cols] + share) / new
        copies.append(
            pltpu.make_async_copy(new_tsdf_ref.at[:, :, cols], new_tsdf_hbm.at[:, :, cols], sems.at[a])
        )
        copies[-1].start()
    copies.append(pltpu.make_async_copy(new_weight_ref, new_weight_hbm, sems.at[4]))
    copies[-1].start()
    for copy in copies:
        copy.wait()


def join(final, old_tsdf, old_weight):
    places = old_weight.shape[0]
    return pl.pallas_call(
        join_kernel,
        out_shape=(
            jax.ShapeDtypeStruct(old_tsdf.shape, f32),
            jax.ShapeDtypeStruct(old_weight.shape, f32),
        ),
        out_specs=(pl.BlockSpec(memory_space=pl.ANY), pl.BlockSpec(memory_space=pl.ANY)),
        scratch_shapes=[
            pltpu.VMEM(((places + 1) * 32, LANES), f32),
            pltpu.VMEM(old_tsdf.shape, f32),
            pltpu.VMEM(old_weight.shape, f32),
            pltpu.VMEM((8, LANES), i32),
            pltpu.SMEM((8, LANES), i32),
            pltpu.SemaphoreType.DMA(()),
            pltpu.SemaphoreType.DMA((5,)),
        ],
        compiler_params=PARAMS,
        name="join",
    )(final, old_tsdf, old_weight)


def local(
    bin_blocks, send_counts, voxel_index, point_sdf, point_weight, point_color, owner_table,
    old_tsdf, old_weight,
):
    packed = pack(
        send_counts, bin_blocks, owner_table, voxel_index, point_weight, point_sdf, point_color
    )
    arrived = lax.all_to_all(packed, "owner", split_axis=0, concat_axis=0, tiled=True)
    sent = route(arrived, lax.axis_size("rep"))
    final = lax.all_to_all(sent, "rep", split_axis=0, concat_axis=0, tiled=True)
    return join(final.reshape(-1, final.shape[2]), old_tsdf, old_weight)


def solution(mesh):
    both = ("owner", "rep")
    placed = (
        P(both),
        P(both, None),
        P(both, None),
        P(both, None),
        P(both, None),
        P(both, None, None),
        P(),
        P(both, None, None),
        P(both, None),
    )
    return jax.shard_map(
        local,
        mesh=mesh,
        in_specs=placed,
        out_specs=(P(both, None, None), P(both, None)),
        check_vma=False,
    )
```

```python
import functools

import jax
import jax.numpy as jnp
from jax import lax
from jax.experimental import pallas as pl
from jax.experimental.pallas import tpu as pltpu
from jax.sharding import PartitionSpec as P

bf16 = jnp.bfloat16
f32 = jnp.float32
i32 = jnp.int32
OWN = 256
LANES = 128
UNIT = 8
WIDE = 8
PARAMS = pltpu.CompilerParams(vmem_limit_bytes=48 << 20)


def ids(shape, dim):
    return lax.broadcasted_iota(i32, shape, dim)


def dot(a, b, dims=((1,), (0,))):
    return lax.dot_general(a, b, (dims, ((), ())), preferred_element_type=f32)


def pack_kernel(*refs):
    sources, out_ref, held, sems = refs[:7], refs[7], refs[8:15], refs[15]
    copies = [
        pltpu.make_async_copy(a, b, sems.at[n]) for n, (a, b) in enumerate(zip(sources, held))
    ]
    for copy in copies:
        copy.start()
    counts_ref, blocks_ref, table_ref, voxel_ref, weight_ref, sdf_ref, color_ref = held
    owners = counts_ref.shape[1]
    bins = blocks_ref.shape[1]
    copies[0].wait()
    counts = jnp.broadcast_to(counts_ref[...], (owners, owners)).astype(f32)
    row, lane = ids((owners, owners), 0), ids((owners, owners), 1)
    ends = jnp.sum(jnp.where(lane <= row, counts, 0.0), axis=1, keepdims=True)
    own = jnp.sum(jnp.where(lane == row, counts, 0.0), axis=1, keepdims=True)
    bin_ids = ids((owners, bins), 1).astype(f32)
    passed = bin_ids >= ends
    target = jnp.sum(jnp.where(passed, 1.0, 0.0), axis=0, keepdims=True)
    before = jnp.sum(jnp.where(passed, own, 0.0), axis=0, keepdims=True)
    slot = (8.0 * target + bin_ids[:1] - before).astype(i32)
    select = jnp.where(ids((8 * owners, bins), 0) == slot, 1.0, 0.0).astype(bf16)
    copies[1].wait()
    copies[2].wait()
    blocks = blocks_ref[...]
    pick = jnp.where(ids((table_ref.shape[0], bins), 0) == blocks // LANES, 1.0, 0.0).astype(bf16)
    table = (table_ref[...] % OWN).astype(f32).astype(bf16)
    found = dot(table, pick, ((0,), (0,)))
    code = 1.0 + jnp.sum(
        jnp.where(ids((LANES, bins), 0) == blocks % LANES, found, 0.0), axis=0, keepdims=True
    )

    def put(channel, values):
        rows = values.reshape(owners, 8, LANES)
        for h in range(2):
            at = (h * 6 + channel) * LANES
            out_ref[:, :, at : at + LANES] = rows[:, 2 * h : 2 * h + 2].astype(bf16)

    coded = dot(select, jnp.broadcast_to(code, (LANES, bins)).astype(bf16), ((1,), (1,)))
    coded = coded.reshape(owners, 8, LANES)
    first = ids((owners, 2, LANES), 2) == 0
    out_ref[:, :, 12 * LANES :] = jnp.where(first, coded[:, :2], coded[:, 2:4]).astype(bf16)
    for copy in copies[3:]:
        copy.wait()
    weight = weight_ref[...].astype(f32)
    features = [(voxel_ref[...] - 256).astype(f32).astype(bf16), weight_ref[...]]
    features.append((weight * sdf_ref[...].astype(f32)).astype(bf16))
    features += [(weight * color_ref[c].astype(f32)).astype(bf16) for c in range(3)]
    for c in range(0, 6, 2):
        pair = dot(select, jnp.concatenate(features[c : c + 2], axis=1))
        put(c, pair[:, :LANES])
        put(c + 1, pair[:, LANES:])


def pack(counts, blocks, table, voxel, weight, sdf, color):
    arrays = (
        counts,
        blocks.reshape(1, -1),
        table.reshape(-1, LANES),
        voxel,
        weight,
        sdf,
        color.transpose(1, 0, 2),
    )
    return pl.pallas_call(
        pack_kernel,
        out_shape=jax.ShapeDtypeStruct((counts.shape[1], 2, 13 * LANES), bf16),
        in_specs=[pl.BlockSpec(memory_space=pltpu.HBM)] * len(arrays),
        scratch_shapes=[pltpu.VMEM(a.shape, a.dtype) for a in arrays]
        + [pltpu.SemaphoreType.DMA((len(arrays),))],
        compiler_params=PARAMS,
        name="pack",
    )(*(pltpu.with_memory_space_constraint(a, pltpu.HBM) for a in arrays))


def rows_of(ref, tile):
    part = ref[:, :, tile * LANES : (tile + 1) * LANES]
    return part.reshape(2 * part.shape[0], LANES)


def both_rows(ref, channel):
    return jnp.concatenate([rows_of(ref, channel), rows_of(ref, 6 + channel)], axis=0)


def route_kernel(in_ref, out_ref):
    replicas, height = out_ref.shape[:2]
    quota = height - 8
    share = OWN // replicas
    tile = rows_of(in_ref, 12)
    count = 2 * tile.shape[0]
    codes = jnp.concatenate(
        [
            dot(jnp.where(ids((8, LANES), 1) == h, 1.0, 0.0).astype(bf16), tile, ((1,), (1,)))[:1]
            for h in range(2)
        ],
        axis=1,
    )
    earlier = jnp.where(ids((LANES, LANES), 0) < ids((LANES, LANES), 1), 1.0, 0.0).astype(bf16)
    quarters = ids((8, LANES), 0).astype(f32)
    total = jnp.zeros((8, 1), f32)
    destinations, spots = [], []
    for g in range(count // LANES):
        code = codes[:, g * LANES : (g + 1) * LANES]
        live = code > 0.5
        quarter = jnp.where(live, jnp.floor((code - 1.0) * (1.0 / share)), 9.0)
        member = jnp.where(quarters == quarter, 1.0, 0.0)
        ahead = dot(member.astype(bf16), earlier) + total
        total = total + jnp.sum(member, axis=1, keepdims=True)
        rank = jnp.sum(ahead * member, axis=0, keepdims=True)
        destinations.append(jnp.where(live, quarter * quota + rank, -1.0))
        spots.append(jnp.where(live, code - quarter * share, 0.0))
    destination = jnp.concatenate(destinations, axis=1).astype(i32)
    spot = jnp.concatenate(spots, axis=1)
    select = jnp.where(ids((replicas * quota, count), 0) == destination, 1.0, 0.0).astype(bf16)
    placed = dot(jnp.broadcast_to(spot, (8, count)).astype(bf16), select, ((1,), (1,)))
    for q in range(replicas):
        out_ref[q, quota:, :LANES] = placed[:, q * quota : (q + 1) * quota].astype(bf16)
        out_ref[q, quota:, LANES:] = jnp.zeros((8, out_ref.shape[2] - LANES), bf16)
    for c in range(0, 6, 2):
        pair = jnp.concatenate([both_rows(in_ref, c), both_rows(in_ref, c + 1)], axis=1)
        moved = dot(select, pair).astype(bf16)
        for q in range(replicas):
            out_ref[q, :quota, c * LANES : (c + 2) * LANES] = moved[q * quota : (q + 1) * quota]


def route(arrived, replicas):
    quota = 4 * arrived.shape[0] // replicas
    return pl.pallas_call(
        route_kernel,
        out_shape=jax.ShapeDtypeStruct((replicas, quota + 8, 6 * LANES), bf16),
        compiler_params=PARAMS,
        name="route",
    )(arrived)


def join_kernel(
    in_ref, tsdf_ref, weight_ref, new_tsdf_hbm, new_weight_hbm,
    sums_ref, new_tsdf_ref, new_weight_ref, plan_ref, plan, sem, sems,
):
    places = weight_ref.shape[0]
    height = 136
    quota = height - 8
    groups = in_ref.shape[0] // height
    units = groups * quota // UNIT
    unit_row, unit_lane = ids((LANES, LANES), 0), ids((LANES, LANES), 1)
    live_units = jnp.zeros((LANES, LANES), f32)
    for r in range(groups):
        code = in_ref[r * height + quota : r * height + height, :LANES].astype(f32)[:1]
        live = jnp.where(code > 0.5, 1.0, 0.0)
        plan_ref[r : r + 1, :] = jnp.where(code > 0.5, code - 1.0, float(places)).astype(i32)
        bins = jnp.sum(live, axis=1, keepdims=True)
        first = ((unit_row - r * (quota // UNIT)) * UNIT).astype(f32)
        here = (unit_row >= r * (quota // UNIT)) & (unit_row < (r + 1) * (quota // UNIT))
        live_units = jnp.where(here & (first < bins), 1.0, live_units)
    plan_ref[groups : groups + 1, :] = jnp.full((1, LANES), places, i32)
    below = jnp.where(unit_lane < unit_row, 1.0, 0.0).astype(bf16)
    rank = dot(below, live_units.astype(bf16))
    chosen = (live_units > 0.5) & (rank == unit_lane.astype(f32))
    listed = jnp.sum(jnp.where(chosen, unit_row.astype(f32) + 1.0, 0.0), axis=0, keepdims=True)
    listed = jnp.where(listed > 0.5, listed - 1.0, float(units))
    plan_ref[groups + 1 : groups + 2, :] = listed.astype(i32)
    number = jnp.sum(live_units, axis=0, keepdims=True)
    plan_ref[groups + 2 : groups + 3, :] = number.astype(i32)
    copy = pltpu.make_async_copy(plan_ref, plan, sem)
    copy.start()
    sums_ref[...] = jnp.zeros_like(sums_ref)
    copy.wait()

    lanes = ids((LANES, LANES), 0).astype(f32).astype(bf16)
    sub = ids((8, LANES), 0)
    one, zero = jnp.ones((), bf16), jnp.zeros((), bf16)

    def halves(tiles, upper, lower, b):
        hot = jnp.where(lanes == jnp.broadcast_to(lower[b : b + 1], (LANES, LANES)), one, zero)
        feature = jnp.zeros((8, LANES), f32)
        for c in range(5):
            value = jnp.broadcast_to(tiles[1 + c][b : b + 1], (8, LANES))
            feature = jnp.where(sub == c, value, feature)
        level = jnp.broadcast_to(upper[b : b + 1], (8, LANES))
        left = [jnp.where(level == a, feature, 0.0) for a in range(4)]
        return hot, jnp.concatenate(left, axis=0).astype(bf16)

    def step(n, carry):
        for u in range(WIDE):
            unit = plan[groups + 1, n * WIDE + u]
            group = unit // (quota // UNIT)
            within = (unit % (quota // UNIT)) * UNIT
            start = jnp.where(unit < units, group * height + within, 0)
            start = pl.multiple_of(start, UNIT)
            tiles = [
                in_ref[pl.ds(start, UNIT), c * LANES : (c + 1) * LANES].astype(f32)
                for c in range(6)
            ]
            voxel = tiles[0] + 256.0
            upper = jnp.floor(voxel * (1.0 / LANES))
            lower = (voxel - upper * float(LANES)).astype(bf16)
            for b in range(0, UNIT, 2):
                hot_a, left_a = halves(tiles, upper, lower, b)
                hot_b, left_b = halves(tiles, upper, lower, b + 1)
                empty = jnp.zeros_like(left_a)
                left = jnp.concatenate(
                    [
                        jnp.concatenate([left_a, empty], axis=1),
                        jnp.concatenate([empty, left_b], axis=1),
                    ],
                    axis=0,
                )
                grids = dot(left, jnp.concatenate([hot_a, hot_b], axis=1), ((1,), (1,)))
                for k in range(2):
                    at = pl.multiple_of(plan[group, within + b + k] * 32, 32)
                    sums_ref[pl.ds(at, 32), :] += grids[k * 32 : (k + 1) * 32]
        return carry

    lax.fori_loop(0, (plan[groups + 2, 0] + WIDE - 1) // WIDE, step, 0)

    copies = []
    for a in range(4):
        cols = slice(a * LANES, (a + 1) * LANES)
        old = weight_ref[:, cols]
        new = old + sums_ref[pl.ds(a * 8, places, stride=32), :]
        new_weight_ref[:, cols] = new
        for c in range(4):
            share = sums_ref[pl.ds(a * 8 + 1 + c, places, stride=32), :]
            new_tsdf_ref[:, c, cols] = (old * tsdf_ref[:, c, cols] + share) / new
        copies.append(
            pltpu.make_async_copy(new_tsdf_ref.at[:, :, cols], new_tsdf_hbm.at[:, :, cols], sems.at[a])
        )
        copies[-1].start()
    copies.append(pltpu.make_async_copy(new_weight_ref, new_weight_hbm, sems.at[4]))
    copies[-1].start()
    for copy in copies:
        copy.wait()


def join(final, old_tsdf, old_weight):
    places = old_weight.shape[0]
    return pl.pallas_call(
        join_kernel,
        out_shape=(
            jax.ShapeDtypeStruct(old_tsdf.shape, f32),
            jax.ShapeDtypeStruct(old_weight.shape, f32),
        ),
        out_specs=(pl.BlockSpec(memory_space=pl.ANY), pl.BlockSpec(memory_space=pl.ANY)),
        scratch_shapes=[
            pltpu.VMEM(((places + 1) * 32, LANES), f32),
            pltpu.VMEM(old_tsdf.shape, f32),
            pltpu.VMEM(old_weight.shape, f32),
            pltpu.VMEM((8, LANES), i32),
            pltpu.SMEM((8, LANES), i32),
            pltpu.SemaphoreType.DMA(()),
            pltpu.SemaphoreType.DMA((5,)),
        ],
        compiler_params=PARAMS,
        name="join",
    )(final, old_tsdf, old_weight)


def local(
    bin_blocks, send_counts, voxel_index, point_sdf, point_weight, point_color, owner_table,
    old_tsdf, old_weight,
):
    packed = pack(
        send_counts, bin_blocks, owner_table, voxel_index, point_weight, point_sdf, point_color
    )
    arrived = lax.all_to_all(packed, "owner", split_axis=0, concat_axis=0, tiled=True)
    sent = route(arrived, lax.axis_size("rep"))
    final = lax.all_to_all(sent, "rep", split_axis=0, concat_axis=0, tiled=True)
    return join(final.reshape(-1, final.shape[2]), old_tsdf, old_weight)


def solution(mesh):
    both = ("owner", "rep")
    placed = (
        P(both),
        P(both, None),
        P(both, None),
        P(both, None),
        P(both, None),
        P(both, None, None),
        P(),
        P(both, None, None),
        P(both, None),
    )
    return jax.shard_map(
        local,
        mesh=mesh,
        in_specs=placed,
        out_specs=(P(both, None, None), P(both, None)),
        check_vma=False,
    )
```

```python
import functools

import jax
import jax.numpy as jnp
from jax import lax
from jax.experimental import pallas as pl
from jax.experimental.pallas import tpu as pltpu
from jax.sharding import PartitionSpec as P

bf16 = jnp.bfloat16
f32 = jnp.float32
i32 = jnp.int32
OWN = 256
LANES = 128
UNIT = 8
WIDE = 8
PARAMS = pltpu.CompilerParams(vmem_limit_bytes=48 << 20)


def ids(shape, dim):
    return lax.broadcasted_iota(i32, shape, dim)


def dot(a, b, dims=((1,), (0,))):
    return lax.dot_general(a, b, (dims, ((), ())), preferred_element_type=f32)


def pack_kernel(*refs):
    sources, out_ref, held, sems = refs[:7], refs[7], refs[8:15], refs[15]
    copies = [
        pltpu.make_async_copy(a, b, sems.at[n]) for n, (a, b) in enumerate(zip(sources, held))
    ]
    for copy in copies:
        copy.start()
    counts_ref, blocks_ref, table_ref, voxel_ref, weight_ref, sdf_ref, color_ref = held
    owners = counts_ref.shape[1]
    bins = blocks_ref.shape[1]
    copies[0].wait()
    counts = jnp.broadcast_to(counts_ref[...], (owners, owners)).astype(f32)
    row, lane = ids((owners, owners), 0), ids((owners, owners), 1)
    ends = jnp.sum(jnp.where(lane <= row, counts, 0.0), axis=1, keepdims=True)
    own = jnp.sum(jnp.where(lane == row, counts, 0.0), axis=1, keepdims=True)
    bin_ids = ids((owners, bins), 1).astype(f32)
    passed = bin_ids >= ends
    target = jnp.sum(jnp.where(passed, 1.0, 0.0), axis=0, keepdims=True)
    before = jnp.sum(jnp.where(passed, own, 0.0), axis=0, keepdims=True)
    slot = (8.0 * target + bin_ids[:1] - before).astype(i32)
    select = jnp.where(ids((8 * owners, bins), 0) == slot, 1.0, 0.0).astype(bf16)
    copies[1].wait()
    copies[2].wait()
    blocks = blocks_ref[...]
    pick = jnp.where(ids((table_ref.shape[0], bins), 0) == blocks // LANES, 1.0, 0.0).astype(bf16)
    table = (table_ref[...] % OWN).astype(f32).astype(bf16)
    found = dot(table, pick, ((0,), (0,)))
    code = 1.0 + jnp.sum(
        jnp.where(ids((LANES, bins), 0) == blocks % LANES, found, 0.0), axis=0, keepdims=True
    )

    def put(channel, values):
        rows = values.reshape(owners, 8, LANES)
        for h in range(2):
            at = (h * 6 + channel) * LANES
            out_ref[:, :, at : at + LANES] = rows[:, 2 * h : 2 * h + 2].astype(bf16)

    coded = dot(select, jnp.broadcast_to(code, (LANES, bins)).astype(bf16), ((1,), (1,)))
    coded = coded.reshape(owners, 8, LANES)
    first = ids((owners, 2, LANES), 2) == 0
    out_ref[:, :, 12 * LANES :] = jnp.where(first, coded[:, :2], coded[:, 2:4]).astype(bf16)
    for copy in copies[3:]:
        copy.wait()
    weight = weight_ref[...].astype(f32)
    features = [(voxel_ref[...] - 256).astype(f32).astype(bf16), weight_ref[...]]
    features.append((weight * sdf_ref[...].astype(f32)).astype(bf16))
    features += [(weight * color_ref[c].astype(f32)).astype(bf16) for c in range(3)]
    for c in range(0, 6, 2):
        pair = dot(select, jnp.concatenate(features[c : c + 2], axis=1))
        put(c, pair[:, :LANES])
        put(c + 1, pair[:, LANES:])


def pack(counts, blocks, table, voxel, weight, sdf, color):
    arrays = (
        counts,
        blocks.reshape(1, -1),
        table.reshape(-1, LANES),
        voxel,
        weight,
        sdf,
        color.transpose(1, 0, 2),
    )
    return pl.pallas_call(
        pack_kernel,
        out_shape=jax.ShapeDtypeStruct((counts.shape[1], 2, 13 * LANES), bf16),
        in_specs=[pl.BlockSpec(memory_space=pltpu.HBM)] * len(arrays),
        scratch_shapes=[pltpu.VMEM(a.shape, a.dtype) for a in arrays]
        + [pltpu.SemaphoreType.DMA((len(arrays),))],
        compiler_params=PARAMS,
        name="pack",
    )(*(pltpu.with_memory_space_constraint(a, pltpu.HBM) for a in arrays))


def rows_of(ref, tile):
    part = ref[:, :, tile * LANES : (tile + 1) * LANES]
    return part.reshape(2 * part.shape[0], LANES)


def both_rows(ref, channel):
    return jnp.concatenate([rows_of(ref, channel), rows_of(ref, 6 + channel)], axis=0)


def route_kernel(in_ref, out_ref, mine_ref):
    replicas, height = out_ref.shape[:2]
    quota = height - 8
    share = OWN // replicas
    tile = rows_of(in_ref, 12)
    count = 2 * tile.shape[0]
    codes = jnp.concatenate(
        [
            dot(jnp.where(ids((8, LANES), 1) == h, 1.0, 0.0).astype(bf16), tile, ((1,), (1,)))[:1]
            for h in range(2)
        ],
        axis=1,
    )
    earlier = jnp.where(ids((LANES, LANES), 0) < ids((LANES, LANES), 1), 1.0, 0.0).astype(bf16)
    quarters = ids((8, LANES), 0).astype(f32)
    total = jnp.zeros((8, 1), f32)
    destinations, spots = [], []
    for g in range(count // LANES):
        code = codes[:, g * LANES : (g + 1) * LANES]
        live = code > 0.5
        quarter = jnp.where(live, jnp.floor((code - 1.0) * (1.0 / share)), 9.0)
        member = jnp.where(quarters == quarter, 1.0, 0.0)
        ahead = dot(member.astype(bf16), earlier) + total
        total = total + jnp.sum(member, axis=1, keepdims=True)
        rank = jnp.sum(ahead * member, axis=0, keepdims=True)
        destinations.append(jnp.where(live, quarter * quota + rank, -1.0))
        spots.append(jnp.where(live, code - quarter * share, 0.0))
    destination = jnp.concatenate(destinations, axis=1).astype(i32)
    spot = jnp.concatenate(spots, axis=1)
    select = jnp.where(ids((replicas * quota, count), 0) == destination, 1.0, 0.0).astype(bf16)
    placed = dot(jnp.broadcast_to(spot, (8, count)).astype(bf16), select, ((1,), (1,)))
    for q in range(replicas):
        out_ref[q, quota:, :LANES] = placed[:, q * quota : (q + 1) * quota].astype(bf16)
        out_ref[q, quota:, LANES:] = jnp.zeros((8, out_ref.shape[2] - LANES), bf16)
    for c in range(0, 6, 2):
        pair = jnp.concatenate([both_rows(in_ref, c), both_rows(in_ref, c + 1)], axis=1)
        moved = dot(select, pair).astype(bf16)
        for q in range(replicas):
            out_ref[q, :quota, c * LANES : (c + 2) * LANES] = moved[q * quota : (q + 1) * quota]
    mine_ref[0] = out_ref[lax.axis_index("rep")]


def route(arrived, replicas):
    quota = 4 * arrived.shape[0] // replicas
    return pl.pallas_call(
        route_kernel,
        out_shape=[jax.ShapeDtypeStruct((n, quota + 8, 6 * LANES), bf16) for n in (replicas, 1)],
        compiler_params=PARAMS,
        name="route",
    )(arrived)


def add_bins(in_ref, sums_ref, plan_ref, plan, sem, skipped, meanwhile):
    groups, height = in_ref.shape[:2]
    quota = height - 8
    spare = sums_ref.shape[0] // 32 - 1
    each = quota // UNIT
    units = groups * each
    unit_row, unit_lane = ids((LANES, LANES), 0), ids((LANES, LANES), 1)
    live_units = jnp.zeros((LANES, LANES), f32)
    for r in range(groups):
        code = in_ref[r, quota:, :LANES].astype(f32)[:1]
        live = jnp.where(code > 0.5, 1.0, 0.0)
        plan_ref[r : r + 1, :] = jnp.where(code > 0.5, code - 1.0, float(spare)).astype(i32)
        bins = jnp.sum(live, axis=1, keepdims=True)
        bins = bins * jnp.where(skipped == r, 0.0, 1.0)
        first = ((unit_row - r * each) * UNIT).astype(f32)
        here = (unit_row >= r * each) & (unit_row < (r + 1) * each)
        live_units = jnp.where(here & (first < bins), 1.0, live_units)
    plan_ref[groups : groups + 1, :] = jnp.full((1, LANES), spare, i32)
    below = jnp.where(unit_lane < unit_row, 1.0, 0.0).astype(bf16)
    rank = dot(below, live_units.astype(bf16))
    chosen = (live_units > 0.5) & (rank == unit_lane.astype(f32))
    listed = jnp.sum(jnp.where(chosen, unit_row.astype(f32) + 1.0, 0.0), axis=0, keepdims=True)
    listed = jnp.where(listed > 0.5, listed - 1.0, float(units))
    plan_ref[groups + 1 : groups + 2, :] = listed.astype(i32)
    number = jnp.sum(live_units, axis=0, keepdims=True)
    plan_ref[groups + 2 : groups + 3, :] = number.astype(i32)
    copy = pltpu.make_async_copy(plan_ref, plan, sem)
    copy.start()
    meanwhile()
    copy.wait()

    lanes = ids((LANES, LANES), 0).astype(f32).astype(bf16)
    sub = ids((8, LANES), 0)
    one, zero = jnp.ones((), bf16), jnp.zeros((), bf16)

    def halves(tiles, upper, lower, b):
        hot = jnp.where(lanes == jnp.broadcast_to(lower[b : b + 1], (LANES, LANES)), one, zero)
        feature = jnp.zeros((8, LANES), f32)
        for c in range(5):
            value = jnp.broadcast_to(tiles[1 + c][b : b + 1], (8, LANES))
            feature = jnp.where(sub == c, value, feature)
        level = jnp.broadcast_to(upper[b : b + 1], (8, LANES))
        left = [jnp.where(level == a, feature, 0.0) for a in range(4)]
        return hot, jnp.concatenate(left, axis=0).astype(bf16)

    def step(n, carry):
        for u in range(WIDE):
            unit = plan[groups + 1, n * WIDE + u]
            group = unit // each
            within = (unit % each) * UNIT
            source = jnp.minimum(group, groups - 1)
            rows = pl.ds(pl.multiple_of(within, UNIT), UNIT)
            tiles = [
                in_ref[source, rows, c * LANES : (c + 1) * LANES].astype(f32) for c in range(6)
            ]
            voxel = tiles[0] + 256.0
            upper = jnp.floor(voxel * (1.0 / LANES))
            lower = (voxel - upper * float(LANES)).astype(bf16)
            for b in range(0, UNIT, 2):
                hot_a, left_a = halves(tiles, upper, lower, b)
                hot_b, left_b = halves(tiles, upper, lower, b + 1)
                empty = jnp.zeros_like(left_a)
                left = jnp.concatenate(
                    [
                        jnp.concatenate([left_a, empty], axis=1),
                        jnp.concatenate([empty, left_b], axis=1),
                    ],
                    axis=0,
                )
                grids = dot(left, jnp.concatenate([hot_a, hot_b], axis=1), ((1,), (1,)))
                for k in range(2):
                    at = pl.multiple_of(plan[group, within + b + k] * 32, 32)
                    sums_ref[pl.ds(at, 32), :] += grids[k * 32 : (k + 1) * 32]
        return carry

    lax.fori_loop(0, (plan[groups + 2, 0] + WIDE - 1) // WIDE, step, 0)


PLAN = [
    pltpu.VMEM((8, LANES), i32),
    pltpu.SMEM((8, LANES), i32),
    pltpu.SemaphoreType.DMA(()),
]


def begin_kernel(in_ref, tsdf_ref, weight_ref, sums_ref, plan_ref, plan, sem):
    places = weight_ref.shape[0]

    def lay():
        sums_ref[...] = jnp.zeros_like(sums_ref)
        for a in range(4):
            cols = slice(a * LANES, (a + 1) * LANES)
            old = weight_ref[:, cols]
            sums_ref[pl.ds(a * 8, places, stride=32), :] = old
            for c in range(4):
                at = pl.ds(a * 8 + 1 + c, places, stride=32)
                sums_ref[at, :] = old * tsdf_ref[:, c, cols]

    add_bins(in_ref, sums_ref, plan_ref, plan, sem, -1, lay)


def begin(mine, old_tsdf, old_weight):
    return pl.pallas_call(
        begin_kernel,
        out_shape=jax.ShapeDtypeStruct(((old_weight.shape[0] + 1) * 32, LANES), f32),
        scratch_shapes=PLAN,
        compiler_params=PARAMS,
        name="begin",
    )(mine, old_tsdf, old_weight)


def join_kernel(
    in_ref, begun_ref, new_tsdf_hbm, new_weight_hbm,
    sums_ref, new_tsdf_ref, new_weight_ref, plan_ref, plan, sem, sems,
):
    places = new_weight_ref.shape[0]

    def clear():
        sums_ref[...] = jnp.zeros_like(sums_ref)

    add_bins(in_ref, sums_ref, plan_ref, plan, sem, lax.axis_index("rep"), clear)
    copies = []
    for a in range(4):
        cols = slice(a * LANES, (a + 1) * LANES)
        at = [pl.ds(a * 8 + c, places, stride=32) for c in range(5)]
        new = begun_ref[at[0], :] + sums_ref[at[0], :]
        new_weight_ref[:, cols] = new
        for c in range(4):
            new_tsdf_ref[:, c, cols] = (begun_ref[at[1 + c], :] + sums_ref[at[1 + c], :]) / new
        copies.append(
            pltpu.make_async_copy(
                new_tsdf_ref.at[:, :, cols], new_tsdf_hbm.at[:, :, cols], sems.at[a]
            )
        )
        copies[-1].start()
    copies.append(pltpu.make_async_copy(new_weight_ref, new_weight_hbm, sems.at[4]))
    copies[-1].start()
    for copy in copies:
        copy.wait()


def join(final, begun, tsdf, weight):
    return pl.pallas_call(
        join_kernel,
        out_shape=(tsdf, weight),
        out_specs=(pl.BlockSpec(memory_space=pl.ANY), pl.BlockSpec(memory_space=pl.ANY)),
        scratch_shapes=[
            pltpu.VMEM(begun.shape, f32),
            pltpu.VMEM(tsdf.shape, f32),
            pltpu.VMEM(weight.shape, f32),
            *PLAN,
            pltpu.SemaphoreType.DMA((5,)),
        ],
        compiler_params=PARAMS,
        name="join",
    )(final, begun)


def local(
    bin_blocks, send_counts, voxel_index, point_sdf, point_weight, point_color, owner_table,
    old_tsdf, old_weight,
):
    packed = pack(
        send_counts, bin_blocks, owner_table, voxel_index, point_weight, point_sdf, point_color
    )
    arrived = lax.all_to_all(packed, "owner", split_axis=0, concat_axis=0, tiled=True)
    sent, mine = route(arrived, lax.axis_size("rep"))
    final = lax.all_to_all(sent, "rep", split_axis=0, concat_axis=0, tiled=True)
    begun = begin(mine, old_tsdf, old_weight)
    shapes = [jax.ShapeDtypeStruct(a.shape, a.dtype) for a in (old_tsdf, old_weight)]
    return join(final, begun, *shapes)


def solution(mesh):
    both = ("owner", "rep")
    placed = (
        P(both),
        P(both, None),
        P(both, None),
        P(both, None),
        P(both, None),
        P(both, None, None),
        P(),
        P(both, None, None),
        P(both, None),
    )
    return jax.shard_map(
        local,
        mesh=mesh,
        in_specs=placed,
        out_specs=(P(both, None, None), P(both, None)),
        check_vma=False,
    )
```

```python
import functools

import jax
import jax.numpy as jnp
from jax import lax
from jax.experimental import pallas as pl
from jax.experimental.pallas import tpu as pltpu
from jax.sharding import PartitionSpec as P

bf16 = jnp.bfloat16
f32 = jnp.float32
i32 = jnp.int32
OWN = 256
LANES = 128
UNIT = 8
WIDE = 8
HALF = 64
DEEP = 40
PART = 16
PARAMS = pltpu.CompilerParams(vmem_limit_bytes=48 << 20)


def ids(shape, dim):
    return lax.broadcasted_iota(i32, shape, dim)


def dot(a, b, dims=((1,), (0,))):
    return lax.dot_general(a, b, (dims, ((), ())), preferred_element_type=f32)


def pack_kernel(*refs):
    sources, out_ref, held, sems = refs[:7], refs[7], refs[8:15], refs[15]
    copies = [
        pltpu.make_async_copy(a, b, sems.at[n]) for n, (a, b) in enumerate(zip(sources, held))
    ]
    for copy in copies:
        copy.start()
    counts_ref, blocks_ref, table_ref, voxel_ref, weight_ref, sdf_ref, color_ref = held
    owners = counts_ref.shape[1]
    bins = blocks_ref.shape[1]
    copies[0].wait()
    counts = jnp.broadcast_to(counts_ref[...], (owners, owners)).astype(f32)
    row, lane = ids((owners, owners), 0), ids((owners, owners), 1)
    ends = jnp.sum(jnp.where(lane <= row, counts, 0.0), axis=1, keepdims=True)
    own = jnp.sum(jnp.where(lane == row, counts, 0.0), axis=1, keepdims=True)
    bin_ids = ids((owners, bins), 1).astype(f32)
    passed = bin_ids >= ends
    target = jnp.sum(jnp.where(passed, 1.0, 0.0), axis=0, keepdims=True)
    before = jnp.sum(jnp.where(passed, own, 0.0), axis=0, keepdims=True)
    position = bin_ids[:1] - before
    second = jnp.where(position > 1.5, 1.0, 0.0)
    slot = (2.0 * target + position + second * (2.0 * owners - 2.0)).astype(i32)
    select = jnp.where(ids((4 * owners, bins), 0) == slot, 1.0, 0.0).astype(bf16)
    copies[1].wait()
    copies[2].wait()
    blocks = blocks_ref[...]
    pick = jnp.where(ids((table_ref.shape[0], bins), 0) == blocks // LANES, 1.0, 0.0).astype(bf16)
    table = (table_ref[...] % OWN).astype(f32).astype(bf16)
    found = dot(table, pick, ((0,), (0,)))
    code = 1.0 + jnp.sum(
        jnp.where(ids((LANES, bins), 0) == blocks % LANES, found, 0.0), axis=0, keepdims=True
    )

    def cut(values, h):
        half = values[h * 2 * owners : (h + 1) * 2 * owners]
        return half.astype(bf16).reshape(owners, 2, LANES)

    def put(channel, values):
        for h in range(2):
            at = (h * 6 + channel) * LANES
            out_ref[:, :, at : at + LANES] = cut(values, h)

    coded = dot(select, jnp.broadcast_to(code, (LANES, bins)).astype(bf16), ((1,), (1,)))
    first = ids((2 * owners, LANES), 1) == 0
    coded = jnp.where(first, coded[: 2 * owners], coded[2 * owners :])
    out_ref[:, :, 12 * LANES :] = cut(coded, 0)
    for copy in copies[3:]:
        copy.wait()
    weight = weight_ref[...].astype(f32)
    features = [(voxel_ref[...] - 256).astype(f32).astype(bf16), weight_ref[...]]
    features.append((weight * sdf_ref[...].astype(f32)).astype(bf16))
    features += [(weight * color_ref[c].astype(f32)).astype(bf16) for c in range(3)]
    for c in range(0, 6, 2):
        pair = dot(select, jnp.concatenate(features[c : c + 2], axis=1))
        put(c, pair[:, :LANES])
        put(c + 1, pair[:, LANES:])


def pack(counts, blocks, table, voxel, weight, sdf, color):
    arrays = (
        counts,
        blocks.reshape(1, -1),
        table.reshape(-1, LANES),
        voxel,
        weight,
        sdf,
        color.transpose(1, 0, 2),
    )
    return pl.pallas_call(
        pack_kernel,
        out_shape=jax.ShapeDtypeStruct((counts.shape[1], 2, 13 * LANES), bf16),
        in_specs=[pl.BlockSpec(memory_space=pltpu.HBM)] * len(arrays),
        scratch_shapes=[pltpu.VMEM(a.shape, a.dtype) for a in arrays]
        + [pltpu.SemaphoreType.DMA((len(arrays),))],
        compiler_params=PARAMS,
        name="pack",
    )(*(pltpu.with_memory_space_constraint(a, pltpu.HBM) for a in arrays))


def rows_of(ref, tile):
    part = ref[:, :, tile * LANES : (tile + 1) * LANES]
    return part.reshape(2 * part.shape[0], LANES)


def both_rows(ref, channel):
    return jnp.concatenate([rows_of(ref, channel), rows_of(ref, 6 + channel)], axis=0)


def route_kernel(in_ref, out_ref):
    replicas, height = out_ref.shape[:2]
    quota = height - 8
    share = OWN // replicas
    tile = rows_of(in_ref, 12)
    count = 2 * tile.shape[0]
    codes = jnp.concatenate(
        [
            dot(jnp.where(ids((8, LANES), 1) == h, 1.0, 0.0).astype(bf16), tile, ((1,), (1,)))[:1]
            for h in range(2)
        ],
        axis=1,
    )
    earlier = jnp.where(ids((LANES, LANES), 0) < ids((LANES, LANES), 1), 1.0, 0.0).astype(bf16)
    quarters = ids((8, LANES), 0).astype(f32)
    total = jnp.zeros((8, 1), f32)
    destinations, spots = [], []
    for g in range(count // LANES):
        code = codes[:, g * LANES : (g + 1) * LANES]
        live = code > 0.5
        quarter = jnp.where(live, jnp.floor((code - 1.0) * (1.0 / share)), 9.0)
        member = jnp.where(quarters == quarter, 1.0, 0.0)
        ahead = dot(member.astype(bf16), earlier) + total
        total = total + jnp.sum(member, axis=1, keepdims=True)
        rank = jnp.sum(ahead * member, axis=0, keepdims=True)
        destinations.append(jnp.where(live, quarter * quota + rank, -1.0))
        spots.append(jnp.where(live, code - quarter * share, 0.0))
    destination = jnp.concatenate(destinations, axis=1).astype(i32)
    spot = jnp.concatenate(spots, axis=1)
    select = jnp.where(ids((replicas * quota, count), 0) == destination, 1.0, 0.0).astype(bf16)
    placed = dot(jnp.broadcast_to(spot, (8, count)).astype(bf16), select, ((1,), (1,)))
    for q in range(replicas):
        out_ref[q, quota:, :LANES] = placed[:, q * quota : (q + 1) * quota].astype(bf16)
        out_ref[q, quota:, LANES:] = jnp.zeros((8, out_ref.shape[2] - LANES), bf16)
    for c in range(0, 6, 2):
        pair = jnp.concatenate([both_rows(in_ref, c), both_rows(in_ref, c + 1)], axis=1)
        moved = dot(select, pair).astype(bf16)
        for q in range(replicas):
            out_ref[q, :quota, c * LANES : (c + 2) * LANES] = moved[q * quota : (q + 1) * quota]


def route(arrived, replicas):
    quota = 4 * arrived.shape[0] // replicas
    return pl.pallas_call(
        route_kernel,
        out_shape=jax.ShapeDtypeStruct((replicas, quota + 8, 6 * LANES), bf16),
        compiler_params=PARAMS,
        name="route",
    )(arrived)


def join_kernel(
    in_ref, tsdf_ref, weight_ref, new_tsdf_hbm, new_weight_hbm,
    sums_ref, new_tsdf_ref, new_weight_ref, plan_ref, plan, sem, sems,
):
    places = weight_ref.shape[0]
    height = 136
    quota = height - 8
    groups = in_ref.shape[0] // height
    units = groups * quota // UNIT
    unit_row, unit_lane = ids((LANES, LANES), 0), ids((LANES, LANES), 1)
    live_units = jnp.zeros((LANES, LANES), f32)
    for r in range(groups):
        code = in_ref[r * height + quota : r * height + height, :LANES].astype(f32)[:1]
        live = jnp.where(code > 0.5, 1.0, 0.0)
        plan_ref[r : r + 1, :] = jnp.where(code > 0.5, code - 1.0, float(places)).astype(i32)
        bins = jnp.sum(live, axis=1, keepdims=True)
        first = ((unit_row - r * (quota // UNIT)) * UNIT).astype(f32)
        here = (unit_row >= r * (quota // UNIT)) & (unit_row < (r + 1) * (quota // UNIT))
        live_units = jnp.where(here & (first < bins), 1.0, live_units)
    plan_ref[groups : groups + 1, :] = jnp.full((1, LANES), places, i32)
    below = jnp.where(unit_lane < unit_row, 1.0, 0.0).astype(bf16)
    rank = dot(below, live_units.astype(bf16))
    chosen = (live_units > 0.5) & (rank == unit_lane.astype(f32))
    listed = jnp.sum(jnp.where(chosen, unit_row.astype(f32) + 1.0, 0.0), axis=0, keepdims=True)
    listed = jnp.where(listed > 0.5, listed - 1.0, float(units))
    plan_ref[groups + 1 : groups + 2, :] = listed.astype(i32)
    number = jnp.sum(live_units, axis=0, keepdims=True)
    plan_ref[groups + 2 : groups + 3, :] = number.astype(i32)
    copy = pltpu.make_async_copy(plan_ref, plan, sem)
    copy.start()
    def lay(row, values):
        for half in range(2):
            at = pl.ds(row + half, places, stride=DEEP)
            sums_ref[at, :HALF] = values[:, half * HALF : (half + 1) * HALF]

    for a in range(4):
        cols = slice(a * LANES, (a + 1) * LANES)
        old = weight_ref[:, cols]
        lay(2 * a, old)
        for c in range(4):
            lay(8 * c + 8 + 2 * a, old * tsdf_ref[:, c, cols])
    copy.wait()

    lanes = ids((HALF, LANES), 0).astype(f32).astype(bf16)
    sub = ids((8, LANES), 0)
    level = sub.astype(f32)
    one, zero = jnp.ones((), bf16), jnp.zeros((), bf16)

    def halves(tiles, upper, lower, b):
        hot = jnp.where(lanes == jnp.broadcast_to(lower[b : b + 1], (HALF, LANES)), one, zero)
        here = jnp.broadcast_to(upper[b : b + 1], (8, LANES)) == level
        rows = [jnp.broadcast_to(tiles[1 + c][b : b + 1], (8, LANES)) for c in range(5)]
        left = [jnp.where(here, row, 0.0) for row in rows]
        return hot, jnp.concatenate(left, axis=0)

    def step(n, carry):
        for u in range(WIDE):
            unit = plan[groups + 1, n * WIDE + u]
            group = unit // (quota // UNIT)
            within = (unit % (quota // UNIT)) * UNIT
            start = jnp.where(unit < units, group * height + within, 0)
            start = pl.multiple_of(start, UNIT)
            tiles = [
                in_ref[pl.ds(start, UNIT), c * LANES : (c + 1) * LANES].astype(f32)
                for c in range(6)
            ]
            voxel = tiles[0] + 256.0
            upper = jnp.floor(voxel * (1.0 / HALF))
            lower = (voxel - upper * float(HALF)).astype(bf16)
            for b in range(0, UNIT, 2):
                hot_a, left_a = halves(tiles, upper, lower, b)
                hot_b, left_b = halves(tiles, upper, lower, b + 1)
                empty = jnp.zeros_like(left_a)
                left = jnp.concatenate(
                    [
                        jnp.concatenate([left_a, empty], axis=1),
                        jnp.concatenate([empty, left_b], axis=1),
                    ],
                    axis=0,
                ).astype(bf16)
                grids = dot(left, jnp.concatenate([hot_a, hot_b], axis=1), ((1,), (1,)))
                for k in range(2):
                    at = pl.multiple_of(plan[group, within + b + k] * DEEP, 8)
                    sums_ref[pl.ds(at, DEEP), :HALF] += grids[k * DEEP : (k + 1) * DEEP]
        return carry

    lax.fori_loop(0, (plan[groups + 2, 0] + WIDE - 1) // WIDE, step, 0)

    def taken(row):
        halves = [sums_ref[pl.ds(row + half, PART, stride=DEEP), :HALF] for half in range(2)]
        return jnp.concatenate(halves, axis=1)

    copies = []
    for first in range(0, places, PART):
        part = slice(first, first + PART)
        for a in range(4):
            cols = slice(a * LANES, (a + 1) * LANES)
            base = first * DEEP + 2 * a
            new = taken(base)
            new_weight_ref[part, cols] = new
            scale = 1.0 / new
            for c in range(4):
                new_tsdf_ref[part, c, cols] = taken(base + 8 * c + 8) * scale
        n = first // PART
        copies.append(
            pltpu.make_async_copy(new_tsdf_ref.at[part], new_tsdf_hbm.at[part], sems.at[2 * n])
        )
        copies.append(
            pltpu.make_async_copy(
                new_weight_ref.at[part], new_weight_hbm.at[part], sems.at[2 * n + 1]
            )
        )
        copies[-2].start()
        copies[-1].start()
    for copy in copies:
        copy.wait()


def join(final, old_tsdf, old_weight):
    places = old_weight.shape[0]
    return pl.pallas_call(
        join_kernel,
        out_shape=(
            jax.ShapeDtypeStruct(old_tsdf.shape, f32),
            jax.ShapeDtypeStruct(old_weight.shape, f32),
        ),
        out_specs=(pl.BlockSpec(memory_space=pl.ANY), pl.BlockSpec(memory_space=pl.ANY)),
        scratch_shapes=[
            pltpu.VMEM(((places + 1) * DEEP, LANES), f32),
            pltpu.VMEM(old_tsdf.shape, f32),
            pltpu.VMEM(old_weight.shape, f32),
            pltpu.VMEM((8, LANES), i32),
            pltpu.SMEM((8, LANES), i32),
            pltpu.SemaphoreType.DMA(()),
            pltpu.SemaphoreType.DMA((2 * places // PART,)),
        ],
        compiler_params=PARAMS,
        name="join",
    )(final, old_tsdf, old_weight)


def local(
    bin_blocks, send_counts, voxel_index, point_sdf, point_weight, point_color, owner_table,
    old_tsdf, old_weight,
):
    packed = pack(
        send_counts, bin_blocks, owner_table, voxel_index, point_weight, point_sdf, point_color
    )
    arrived = lax.all_to_all(packed, "owner", split_axis=0, concat_axis=0, tiled=True)
    sent = route(arrived, lax.axis_size("rep"))
    final = lax.all_to_all(sent, "rep", split_axis=0, concat_axis=0, tiled=True)
    return join(final.reshape(-1, final.shape[2]), old_tsdf, old_weight)


def solution(mesh):
    both = ("owner", "rep")
    placed = (
        P(both),
        P(both, None),
        P(both, None),
        P(both, None),
        P(both, None),
        P(both, None, None),
        P(),
        P(both, None, None),
        P(both, None),
    )
    return jax.shard_map(
        local,
        mesh=mesh,
        in_specs=placed,
        out_specs=(P(both, None, None), P(both, None)),
        check_vma=False,
    )
```
